32 devices in a mesh: section: 4 (over z), head: 8 (over y, x, core).
Axes of the slice: x: 2, y: 2, z: 4, core: 2. Of those that a mesh axis runs over, the one named last changes fastest.
Arguments:
- section_inputs: bfloat16 [4, 256, 1024], P('section'), may hold values from -6 to 6
- section_cotangents: bfloat16 [4, 256, 1024], P('section'), may hold values from -6 to 6
- fresh_tokens: bfloat16 [2, 256, 1024], replicated, may hold values from -6 to 6
- fresh_cotangents: bfloat16 [2, 256, 1024], replicated, may hold values from -6 to 6
- norm_gain: float32 [4, 1024], P('section'), may hold values from 0.1 to 1.9
- query_weight: bfloat16 [4, 1024, 16384], P('section', None, 'head'), as said below
- key_weight: bfloat16 [4, 1024, 16384], P('section', None, 'head'), may hold values from -0.1875 to 0.1875
- value_weight: bfloat16 [4, 1024, 16384], P('section', None, 'head'), may hold values from -0.1875 to 0.1875
- out_weight: bfloat16 [4, 16384, 1024], P('section', 'head'), may hold values from -0.1875 to 0.1875
- saved_inputs: bfloat16 [4, 4, 256, 1024], P('section', None, None, 'head'), may hold values from -6 to 6
- reload_slot: int32 [2, 4], replicated, may hold values from 0 to 3
Outputs:
- next_inputs: bfloat16 [4, 256, 1024], P('section')
- next_cotangents: bfloat16 [4, 256, 1024], P('section')
- saved_after: bfloat16 [4, 4, 256, 1024], P('section', None, None, 'head')
- query_grad: bfloat16 [4, 1024, 16384], P('section', None, 'head')
- key_grad: bfloat16 [4, 1024, 16384], P('section', None, 'head')
- value_grad: bfloat16 [4, 1024, 16384], P('section', None, 'head')
- out_grad: bfloat16 [4, 16384, 1024], P('section', 'head')
- gain_grad: float32 [4, 1024], P('section', 'head')
The draws below stay inside these ranges and needn't reach their ends.
Inputs may be any that keep to these rules, and one draw needn't show every extreme that they name: `query_weight`: independent entries.
All inputs are finite; a program needn't handle non-finite values.
Results may differ from the reference program's by a relative error of at most 0.015.
The reference program's roundings to bfloat16 on the way count: a program that leaves them out, or rounds other values in their place, can miss the bound.
Values may be sent and summed in bfloat16 or wider, within the bound.
A program may use at most 128 MiB of HBM per device.

```python
import math
import jax
import jax.numpy as jnp
from jax import lax

D = 1024
HEADS = 128
DK = 128
MB = 256
SLOTS = 4
TICKS = 2
SECTIONS = 4


def draw_query_weight(key, part):
    base = jax.random.normal(jax.random.fold_in(key, 11), (SECTIONS, D, HEADS * DK), jnp.float32) / math.sqrt(D)
    return base.astype(jnp.bfloat16)


def place_ends(drawn, key, low, largest):
    shape = drawn.shape
    index_at = [jax.random.randint(jax.random.fold_in(key, axis), (), 0, shape[axis]) for axis in range(len(shape))]
    drawn = drawn.at[tuple(index_at)].set(low)
    longest = shape.index(max(shape))
    index_at[longest] = (index_at[longest] + 1) % shape[longest]
    return drawn.at[tuple(index_at)].set(largest)


def block_levels(own_key, extent, pieces, least, largest):
    gain = 1.0
    for dim, blocks in pieces:
        draws = jax.random.uniform(jax.random.fold_in(jax.random.fold_in(own_key, 6), dim), (blocks,), jnp.float32, least / len(pieces), largest / len(pieces))
        gain = gain * jnp.repeat(jnp.exp(draws), extent[dim] // blocks).reshape((-1,) + (1,) * (len(extent) - 1 - dim))
    return gain


def gaussian(rng, shape, width, most, pieces=(), kind=jnp.bfloat16):
    values = width * jax.random.normal(rng, shape, jnp.float32)
    if pieces:
        values = values * block_levels(rng, shape, pieces, -0.22, 0.18)
    return jnp.clip(values, -most, most).astype(kind)


def setup_inputs(seed: int = 0) -> dict:
    arg_keys = jax.random.split(jax.random.key(seed), 12)
    section_inputs = gaussian(arg_keys[0], (SECTIONS, MB, D), 1.0, 6.0, ((0, 4),))
    section_cotangents = gaussian(arg_keys[1], (SECTIONS, MB, D), 1.0, 6.0, ((0, 4),))
    fresh_tokens = gaussian(arg_keys[2], (TICKS, MB, D), 1.0, 6.0)
    fresh_cotangents = gaussian(arg_keys[3], (TICKS, MB, D), 1.0, 6.0)
    norm_gain = jnp.clip(1.0 + 0.18 * jax.random.normal(arg_keys[4], (SECTIONS, D), jnp.float32), 0.1, 1.9)
    query_weight = draw_query_weight(jax.random.fold_in(arg_keys[11], 71), 0)
    key_weight = gaussian(arg_keys[6], (SECTIONS, D, HEADS * DK), D ** -0.5, 0.1875, ((0, 4), (2, 8)))
    value_weight = gaussian(arg_keys[7], (SECTIONS, D, HEADS * DK), D ** -0.5, 0.1875, ((0, 4), (2, 8)))
    out_weight = gaussian(arg_keys[8], (SECTIONS, HEADS * DK, D), (HEADS * DK // 16) ** -0.5, 0.1875, ((0, 4), (1, 8)))
    saved_inputs = gaussian(arg_keys[9], (SECTIONS, SLOTS, MB, D), 1.0, 6.0, ((0, 4), (3, 8)))
    reload_slot = place_ends(jax.random.randint(arg_keys[10], (TICKS, SECTIONS), 0, SLOTS), jax.random.fold_in(arg_keys[10], 1), 0, SLOTS - 1).astype(jnp.int32)
    return {"section_inputs": section_inputs, "section_cotangents": section_cotangents, "fresh_tokens": fresh_tokens, "fresh_cotangents": fresh_cotangents, "norm_gain": norm_gain, "query_weight": query_weight, "key_weight": key_weight, "value_weight": value_weight, "out_weight": out_weight, "saved_inputs": saved_inputs, "reload_slot": reload_slot}


epsilon = 1e-06

def normalize(rows, gain_row):
    floats = rows.astype(jnp.float32)
    inverse = lax.rsqrt(lax.optimization_barrier(jnp.mean(floats * floats, axis=-1, keepdims=True)) + epsilon)
    unit_rows = floats * inverse
    return ((unit_rows * gain_row).astype(jnp.bfloat16), unit_rows, inverse)

def split_heads(rows):
    return rows.reshape(rows.shape[0], -1, DK).astype(jnp.float32)

def attend(normed, query_part, key_part, value_part):
    queries = jnp.dot(normed, query_part, preferred_element_type=jnp.float32).astype(jnp.bfloat16)
    key_rows = jnp.dot(normed, key_part, preferred_element_type=jnp.float32).astype(jnp.bfloat16)
    value_rows = jnp.dot(normed, value_part, preferred_element_type=jnp.float32).astype(jnp.bfloat16)
    scores = jnp.einsum('qhd,khd->hqk', split_heads(queries), split_heads(key_rows)) * DK ** (-0.5)
    highest = lax.optimization_barrier(jnp.max(scores, axis=-1, keepdims=True))
    exponent = jnp.exp(scores - highest)
    softmax_rows = exponent / lax.optimization_barrier(jnp.sum(exponent, axis=-1, keepdims=True))
    softmax_low = softmax_rows.astype(jnp.bfloat16)
    context = jnp.einsum('hqk,khd->qhd', softmax_low.astype(jnp.float32), split_heads(value_rows))
    context = context.astype(jnp.bfloat16).reshape(normed.shape[0], -1)
    return (queries, key_rows, value_rows, softmax_rows, softmax_low, context)

def forward_layer(rows, gain_row, query_part, key_part, value_part, out_part):
    normed, unit_rows, inverse = normalize(rows, gain_row)
    context = attend(normed, query_part, key_part, value_part)[5]
    total = rows.astype(jnp.float32) + jnp.dot(context, out_part, preferred_element_type=jnp.float32)
    return total.astype(jnp.bfloat16)

def backward_layer(rows, upstream, gain_row, query_part, key_part, value_part, out_part):
    normed, unit_rows, inverse = normalize(rows, gain_row)
    queries, key_rows, value_rows, softmax_rows, softmax_low, context = attend(normed, query_part, key_part, value_part)
    token_count = rows.shape[0]
    out_term = jnp.dot(context.T, upstream, preferred_element_type=jnp.float32)
    context_grad = jnp.dot(upstream, out_part.T, preferred_element_type=jnp.float32).astype(jnp.bfloat16)
    softmax_grad = jnp.einsum('qhd,khd->hqk', split_heads(context_grad), split_heads(value_rows))
    value_rows_grad = jnp.einsum('hqk,qhd->khd', softmax_low.astype(jnp.float32), split_heads(context_grad))
    value_rows_grad = value_rows_grad.astype(jnp.bfloat16).reshape(token_count, -1)
    inner = lax.optimization_barrier(jnp.sum(softmax_rows * softmax_grad, axis=-1, keepdims=True))
    score_grad = (softmax_rows * (softmax_grad - inner) * DK ** (-0.5)).astype(jnp.bfloat16).astype(jnp.float32)
    queries_grad = jnp.einsum('hqk,khd->qhd', score_grad, split_heads(key_rows)).astype(jnp.bfloat16).reshape(token_count, -1)
    key_rows_grad = jnp.einsum('hqk,qhd->khd', score_grad, split_heads(queries)).astype(jnp.bfloat16).reshape(token_count, -1)
    query_term = jnp.dot(normed.T, queries_grad, preferred_element_type=jnp.float32)
    key_term = jnp.dot(normed.T, key_rows_grad, preferred_element_type=jnp.float32)
    value_term = jnp.dot(normed.T, value_rows_grad, preferred_element_type=jnp.float32)
    normed_grad = jnp.dot(queries_grad, query_part.T, preferred_element_type=jnp.float32)
    normed_grad = normed_grad + jnp.dot(key_rows_grad, key_part.T, preferred_element_type=jnp.float32)
    normed_grad = normed_grad + jnp.dot(value_rows_grad, value_part.T, preferred_element_type=jnp.float32)
    gain_term = lax.optimization_barrier(jnp.sum(normed_grad * unit_rows, axis=0))
    unit_grad = normed_grad * gain_row
    along = lax.optimization_barrier(jnp.mean(unit_grad * unit_rows, axis=-1, keepdims=True))
    returned = (upstream.astype(jnp.float32) + inverse * (unit_grad - unit_rows * along)).astype(jnp.bfloat16)
    return (returned, (query_term, key_term, value_term, out_term, gain_term))

def reference(section_inputs, section_cotangents, fresh_tokens, fresh_cotangents, norm_gain, query_weight, key_weight, value_weight, out_weight, saved_inputs, reload_slot):
    count = section_inputs.shape[0]
    stores = [saved_inputs[number] for number in range(count)]
    produced = [[None] * TICKS for number in range(count)]
    loaded = [[None] * TICKS for number in range(count)]
    for section_number in range(count):
        row_store = stores[count - 1 - section_number]
        for tick_number in range(TICKS):
            if tick_number == 0:
                current = section_inputs[section_number]
            elif section_number == 0:
                current = fresh_tokens[tick_number - 1]
            else:
                current = produced[section_number - 1][tick_number - 1]
            slot = reload_slot[tick_number, section_number]
            loaded[section_number][tick_number] = lax.dynamic_index_in_dim(row_store, slot, 0, keepdims=False)
            row_store = lax.dynamic_update_index_in_dim(row_store, current, slot, 0)
            produced[section_number][tick_number] = forward_layer(current, norm_gain[section_number], query_weight[section_number], key_weight[section_number], value_weight[section_number], out_weight[section_number])
        stores[count - 1 - section_number] = row_store
    returned = [[None] * TICKS for number in range(count)]
    grads = [None] * count
    for section_number in range(count - 1, -1, -1):
        sums = None
        for tick_number in range(TICKS):
            if tick_number == 0:
                upstream = section_cotangents[section_number]
            elif section_number == count - 1:
                upstream = fresh_cotangents[tick_number - 1]
            else:
                upstream = returned[section_number + 1][tick_number - 1]
            result, terms = backward_layer(loaded[section_number][tick_number], upstream, norm_gain[section_number], query_weight[section_number], key_weight[section_number], value_weight[section_number], out_weight[section_number])
            returned[section_number][tick_number] = result
            sums = terms if sums is None else tuple((a + b for a, b in zip(sums, terms)))
        grads[section_number] = sums
    next_inputs = jnp.stack([fresh_tokens[TICKS - 1]] + [produced[number - 1][TICKS - 1] for number in range(1, count)])
    next_cotangents = jnp.stack([returned[number + 1][TICKS - 1] for number in range(count - 1)] + [fresh_cotangents[TICKS - 1]])
    saved_after = jnp.stack(stores)
    query_grad = jnp.stack([grads[number][0] for number in range(count)]).astype(jnp.bfloat16)
    key_grad = jnp.stack([grads[number][1] for number in range(count)]).astype(jnp.bfloat16)
    value_grad = jnp.stack([grads[number][2] for number in range(count)]).astype(jnp.bfloat16)
    out_grad = jnp.stack([grads[number][3] for number in range(count)]).astype(jnp.bfloat16)
    gain_grad = jnp.stack([grads[number][4] for number in range(count)])
    return (next_inputs, next_cotangents, saved_after, query_grad, key_grad, value_grad, out_grad, gain_grad)
```

```python
import functools
import math

import jax
import jax.numpy as jnp
from jax import lax
from jax.experimental import pallas as pl
from jax.experimental.pallas import tpu as pltpu
from jax.sharding import PartitionSpec as P

DK = 128
TICKS = 2
CORES = 2
EPSILON = 1e-06
SCALE = DK ** (-0.5)
ONES = (((1,), (1,)), ((), ()))
LOW = jnp.bfloat16
HIGH = jnp.float32
FORWARD_HEADS = 8
BACKWARD_HEADS = 4
CHUNKS = 4


def normalize(rows, gain_row):
    floats = rows.astype(HIGH)
    inverse = lax.rsqrt(jnp.mean(floats * floats, axis=-1, keepdims=True) + EPSILON)
    unit_rows = floats * inverse
    return ((unit_rows * gain_row).astype(LOW), unit_rows, inverse)


def dot(a, b, dims=(((1,), (0,)), ((), ()))):
    return lax.dot_general(a, b, dims, preferred_element_type=HIGH)


def low_dot(a, b, dims=(((1,), (0,)), ((), ()))):
    return dot(a, b, dims).astype(LOW)


def softmax_over(scores, axis):
    shifted = scores - jnp.max(scores, axis=axis, keepdims=True)
    exponent = jnp.exp2(shifted * (SCALE * math.log2(math.e)))
    return exponent * (1.0 / jnp.sum(exponent, axis=axis, keepdims=True))


def ticks_kernel(
    heads, sections,
    slots, x0, g0, fresh_x, fresh_g, gain_hbm, wq_hbm, wk_hbm, wv_hbm, wo_hbm, store_hbm,
    x2, g2, store_out, gain_out, wq_grad, wk_grad, turned, vg, ctx_turned, gcat,
    wq, wk, wv, wo, xs, gain, store, fresh, blocks, b_full, held, shares, arrived,
    normed, ctx, qg_turned, kg, parts, pair_in, rs_out, rs_in, hop_out, gains, gains_in,
    load_sem, weight_sem, sent, got, pair_sent, pair_got,
):
    me, section = lax.axis_index("head"), lax.axis_index("section")
    chips = heads // CORES
    core, chip = lax.rem(me, CORES), me // CORES
    partner = me + 1 - 2 * core
    chip_peers = [lax.rem(chip + d, chips) * CORES + core for d in range(1, chips)]
    mirror = sections - 1 - section
    ahead = lax.rem(section + 1, sections)
    back = lax.rem(section + sections - 1, sections)
    count, depth = x0.shape
    inner = wq.shape[1]
    half = count // CORES
    share = count // heads
    width = store.shape[2]
    chunk = depth // CHUNKS

    def aligned(start, size):
        return pl.ds(pl.multiple_of(start, size), size)

    own = aligned(core * half + chip * share, share)
    own_half = aligned(core * half, half)
    other_half = aligned((1 - core) * half, half)

    loads = [
        pltpu.make_async_copy(source, target, load_sem.at[i])
        for i, (source, target) in enumerate(
            [
                (x0, xs.at[0]),
                (gain_hbm, gain),
                (store_hbm, store),
                (g0, gcat.at[pl.ds(0, count)]),
                (fresh_x.at[0, own], fresh.at[0]),
                (fresh_g.at[0, own], fresh.at[1]),
                (fresh_x.at[1, own], fresh.at[2]),
                (fresh_g.at[1, own], fresh.at[3]),
            ]
        )
    ]
    group_width = min(FORWARD_HEADS * DK, inner)
    groups = inner // group_width
    weight_loads = []
    for i in range(groups):
        piece = pl.ds(i * group_width, group_width)
        weight_loads.append(
            [
                pltpu.make_async_copy(w_hbm.at[:, piece], w.at[:, piece], weight_sem.at[i, n])
                for n, (w_hbm, w) in enumerate(((wq_hbm, wq), (wk_hbm, wk), (wv_hbm, wv)))
            ]
        )
    out_load = pltpu.make_async_copy(wo_hbm, wo, weight_sem.at[0, 3])
    for copy in loads[:3]:
        copy.start()
    for copies in weight_loads:
        for copy in copies:
            copy.start()
    out_load.start()
    for copy in loads[3:]:
        copy.start()

    barrier = pltpu.get_barrier_semaphore()
    for d in range(1, heads):
        pl.semaphore_signal(barrier, inc=1, device_id={"head": lax.rem(me + d, heads)})
    for other in (ahead, back, mirror):
        pl.semaphore_signal(barrier, inc=1, device_id={"section": other})
    pl.semaphore_wait(barrier, heads - 1 + 3)

    sends = []

    def remote(source, target, s, r, where):
        return pltpu.make_async_remote_copy(
            src_ref=source,
            dst_ref=target,
            send_sem=s,
            recv_sem=r,
            device_id=where,
            device_id_type=pl.DeviceIdType.MESH,
        )

    counter = [0]

    def sending(source, target, where):
        i = counter[0]
        counter[0] += 1
        return remote(source, target, sent.at[i], got.at[i], where)

    def go(copy):
        copy.start()
        sends.append(copy)

    def share_of(x, target):
        for i in range(heads):
            @pl.when(me == i)
            def _():
                target[...] = x[:, i * width : (i + 1) * width]

    mirror_copies = {}

    def mirror_send(name, source, target):
        mirror_copies[name] = sending(source, target, {"section": mirror})
        go(mirror_copies[name])

    block_copies = {}

    def reload_start(t):
        held[t] = store[slots[t, mirror]]
        mirror_send(("held", t), held.at[t], blocks.at[t, core, chip])

    def reload_spread(t):
        mirror_copies["held", t].wait_recv()
        own_block = blocks.at[t, core, chip]
        block_copies[t] = [sending(own_block, own_block, {"head": peer}) for peer in chip_peers]
        for copy in block_copies[t]:
            go(copy)

    def reload_pair(t):
        for copy in block_copies[t]:
            copy.wait_recv()
        pair = sending(blocks.at[t, core], blocks.at[t, core], {"head": partner})
        block_copies[t] = [pair]
        go(pair)

    def reload_finish(t):
        block_copies[t][0].wait_recv()
        block = jnp.concatenate(
            [blocks[t, i % CORES, i // CORES] for i in range(heads)], axis=1
        )
        if t:
            first = jnp.broadcast_to(slots[0, section], block.shape)
            second = jnp.broadcast_to(slots[1, section], block.shape)
            block = jnp.where(first == second, xs[0], block)
        b_full[t] = block

    class Chain:
        def __init__(self, number, target):
            self.number, self.target = number, target
            self.tick, self.backward = number // 2, number % 2
            self.pairs = []

        def part(self, j, value):
            n = self.number
            columns = pl.ds(j * chunk, chunk)
            parts[n, :, j * chunk : (j + 1) * chunk] = value.astype(LOW)
            copy = remote(
                parts.at[n, other_half, columns],
                pair_in.at[n, :, columns],
                pair_sent.at[n, j],
                pair_got.at[n, j],
                {"head": partner},
            )
            go(copy)
            self.pairs.append(copy)

        def scatter(self):
            n = self.number
            for copy in self.pairs:
                copy.wait_recv()
            total = parts[n, own_half, :].astype(HIGH) + pair_in[n].astype(HIGH)
            rs_out[n] = total.astype(LOW)
            self.rs = []
            for d, peer in enumerate(chip_peers):
                rows = aligned(lax.rem(chip + d + 1, chips) * share, share)
                self.rs.append(sending(rs_out.at[n, rows], rs_in.at[n, d], {"head": peer}))
                go(self.rs[-1])

        def hop(self):
            n, t = self.number, self.tick
            for copy in self.rs:
                copy.wait_recv()
            mine = aligned(chip * share, share)
            total = parts[n, own, :].astype(HIGH) + pair_in[n, mine, :].astype(HIGH)
            for d in range(chips - 1):
                total += rs_in[n, d].astype(HIGH)
            if self.backward:
                normed_rows, unit_rows, inverse = normalize(b_full[t, own, :], gain[...])
                unit_grad = total * gain[...]
                along = jnp.mean(unit_grad * unit_rows, axis=-1, keepdims=True)
                upstream = gcat[aligned(t * count + core * half + chip * share, share), :]
                result = upstream.astype(HIGH) + inverse * (unit_grad - unit_rows * along)
                products = total * unit_rows
                term = products[:8]
                for start in range(8, share, 8):
                    term += products[start : start + 8]
                self.gain_term = term
                where, sender, receiver = back, section != 0, section != sections - 1
            else:
                result = xs[t, own, :].astype(HIGH) + total
                where, sender, receiver = ahead, section != sections - 1, section != 0
            hop_out[n] = result.astype(LOW)
            self.hopping = sending(hop_out.at[n], self.target(own_start, share), {"section": where})
            self.sender, self.receiver = sender, receiver

            @pl.when(sender)
            def _():
                self.hopping.start()

        def gather(self):
            block = self.target(own_start, share)

            @pl.when(self.receiver)
            def _():
                self.hopping.wait_recv()

            @pl.when(jnp.logical_not(self.receiver))
            def _():
                block[...] = fresh[self.number]

            self.ag = [sending(block, block, {"head": peer}) for peer in chip_peers]
            for copy in self.ag:
                go(copy)

        def pair(self):
            for copy in self.ag:
                copy.wait_recv()
            block = self.target(core * half, half)
            self.last = sending(block, block, {"head": partner})
            go(self.last)

        def finish(self):
            self.last.wait_recv()

        def drain(self):
            @pl.when(self.sender)
            def _():
                self.hopping.wait_send()

    own_start = core * half + chip * share
    chains = [
        Chain(0, lambda start, size: xs.at[1, aligned(start, size)]),
        Chain(1, lambda start, size: gcat.at[aligned(count + start, size)]),
        Chain(2, lambda start, size: x2.at[aligned(start, size)]),
        Chain(3, lambda start, size: g2.at[aligned(start, size)]),
    ]

    pending = []

    def breathe():
        if pending:
            pending.pop(0)()

    def flush():
        while pending:
            breathe()

    def forward(t, before_group):
        normed[...] = normalize(xs[t], gain[...])[0]
        for i in range(groups):
            before_group(i)
            piece = slice(i * group_width, (i + 1) * group_width)
            n = normed[...]
            queries, key_rows, value_rows = (low_dot(n, w[:, piece]) for w in (wq, wk, wv))
            for start in range(0, group_width, DK):
                head = slice(start, start + DK)
                soft = softmax_over(dot(queries[:, head], key_rows[:, head], ONES), -1).astype(LOW)
                place = slice(i * group_width + start, i * group_width + start + DK)
                ctx[:, place] = low_dot(soft, value_rows[:, head])
            breathe()
        if t == 0:
            out_load.wait()
        for j in range(CHUNKS):
            chains[2 * t].part(j, dot(ctx[...], wo[:, j * chunk : (j + 1) * chunk]))

    def backward(t):
        step = min(BACKWARD_HEADS * DK, inner)
        tokens = slice(t * count, (t + 1) * count)
        normed[...] = normalize(b_full[t], gain[...])[0]
        turned[:, tokens] = normed[...].T
        for i in range(inner // step):
            piece = slice(i * step, (i + 1) * step)
            n = normed[...]
            queries, key_rows, value_rows = (low_dot(n, w[:, piece]) for w in (wq, wk, wv))
            ctx_grad = low_dot(gcat[tokens, :], wo[piece, :], ONES)
            for start in range(0, step, DK):
                head = slice(start, start + DK)
                place = slice(i * step + start, i * step + start + DK)
                q, k, v, c = (a[:, head] for a in (queries, key_rows, value_rows, ctx_grad))
                soft = softmax_over(dot(k, q, ONES), 0)
                soft_low = soft.astype(LOW)
                ctx_turned[place, tokens] = low_dot(v.T, soft_low)
                soft_grad = dot(v, c, ONES)
                vg[tokens, place] = low_dot(soft_low, c)
                inside = jnp.sum(soft * soft_grad, axis=0, keepdims=True)
                score_grad = (soft * (soft_grad - inside) * SCALE).astype(LOW)
                qg_turned[place, tokens] = low_dot(k.T, score_grad)
                kg[tokens, place] = low_dot(score_grad, q)
            breathe()
        for j in range(CHUNKS):
            rows = slice(j * chunk, (j + 1) * chunk)
            grad = dot(wq[rows, :], qg_turned[:, tokens])
            grad += dot(wk[rows, :], kg[tokens, :], ONES)
            grad += dot(wv[rows, :], vg[tokens, :], ONES)
            chains[2 * t + 1].part(j, grad.T)

    loads[2].wait()
    reload_start(0)
    loads[0].wait()
    loads[1].wait()
    share_of(xs.at[0], shares.at[0])

    def first_weights(i):
        for copy in weight_loads[i]:
            copy.wait()

    def spread_first():
        reload_spread(0)
        reload_start(1)
        mirror_send(("share", 0), shares.at[0], arrived.at[0])

    pending[:] = [spread_first, lambda: reload_pair(0)]
    forward(0, first_weights)
    flush()
    reload_finish(0)
    for copy in loads[3:]:
        copy.wait()

    def both(*calls):
        def run():
            for call in calls:
                call()
        return run

    chain = chains[0]
    pending[:] = [
        both(chain.scatter, lambda: reload_spread(1)),
        both(chain.hop, lambda: reload_pair(1)),
        both(chain.gather, lambda: reload_finish(1)),
        chain.pair,
    ]
    backward(0)
    flush()
    chain.finish()
    share_of(xs.at[1], shares.at[1])
    mirror_send(("share", 1), shares.at[1], arrived.at[1])

    chain = chains[1]
    pending[:] = [chain.scatter, chain.hop, chain.gather, chain.pair]
    forward(1, lambda i: None)
    flush()
    chain.finish()

    chain = chains[2]
    pending[:] = [chain.scatter, chain.hop, chain.gather, chain.pair, chain.finish]
    backward(1)
    flush()

    def store_update():
        for t in range(TICKS):
            mirror_copies["share", t].wait_recv()
        first = jnp.broadcast_to(slots[0, mirror], (count, width))
        second = jnp.broadcast_to(slots[1, mirror], (count, width))
        for j in range(store.shape[0]):
            value = jnp.where(first == j, arrived[0], store[j])
            store_out[j] = jnp.where(second == j, arrived[1], value)

    gain_copies = []

    def gain_send():
        total = chains[1].gain_term + chains[3].gain_term
        for i in range(heads):
            gains[i] = total[:, i * width : (i + 1) * width]
        for d in range(1, heads):
            peer = lax.rem(me + d, heads)
            gain_copies.append(sending(gains.at[peer], gains_in.at[d - 1], {"head": peer}))
            go(gain_copies[-1])

    def gain_finish():
        total = gains[me]
        for copy in gain_copies:
            copy.wait_recv()
        for d in range(heads - 1):
            total += gains_in[d]
        gain_out[...] = jnp.sum(total, axis=0, keepdims=True)

    chain = chains[3]
    pending[:] = [
        both(chain.scatter, store_update),
        both(chain.hop, gain_send),
        chain.gather,
        both(chain.pair, gain_finish),
    ]
    step = min(4 * DK, inner)
    for i in range(inner // step):
        piece = slice(i * step, (i + 1) * step)
        wq_grad[:, piece] = low_dot(turned[...], qg_turned[piece, :], ONES)
        wk_grad[:, piece] = low_dot(turned[...], kg[:, piece])
        breathe()
    flush()
    chain.finish()
    for copy in sends:
        copy.wait_send()
    for chain in chains:
        chain.drain()


def run_ticks(slots, x0, g0, fresh_x, fresh_g, gain, wq, wk, wv, wo, store):
    heads, sections = lax.axis_size("head"), lax.axis_size("section")
    count, depth = x0.shape
    inner = wq.shape[1]
    slot_count, _, width = store.shape
    chips = heads // CORES
    half, share = count // CORES, count // heads
    groups = inner // min(FORWARD_HEADS * DK, inner)
    peers = chips - 1
    copies = 4 + 2 * (peers + 1) + 4 * (2 * peers + 2) + heads - 1
    anywhere = pl.BlockSpec(memory_space=pl.ANY)
    in_vmem = pl.BlockSpec(memory_space=pltpu.VMEM)
    dma = pltpu.SemaphoreType.DMA
    vmem = pltpu.VMEM
    shape = jax.ShapeDtypeStruct
    return pl.pallas_call(
        functools.partial(ticks_kernel, heads, sections),
        in_specs=[pl.BlockSpec(memory_space=pltpu.SMEM)] + [anywhere] * 10,
        out_specs=[in_vmem] * 10,
        out_shape=[
            shape((count, depth), LOW),
            shape((count, depth), LOW),
            shape(store.shape, LOW),
            shape((1, width), HIGH),
            shape((depth, inner), LOW),
            shape((depth, inner), LOW),
            shape((depth, TICKS * count), LOW),
            shape((TICKS * count, inner), LOW),
            shape((inner, TICKS * count), LOW),
            shape((TICKS * count, depth), LOW),
        ],
        scratch_shapes=[
            vmem((depth, inner), LOW),
            vmem((depth, inner), LOW),
            vmem((depth, inner), LOW),
            vmem((inner, depth), LOW),
            vmem((TICKS, count, depth), LOW),
            vmem((1, depth), HIGH),
            vmem(store.shape, LOW),
            vmem((4, share, depth), LOW),
            vmem((TICKS, CORES, chips, count, width), LOW),
            vmem((TICKS, count, depth), LOW),
            vmem((TICKS, count, width), LOW),
            vmem((TICKS, count, width), LOW),
            vmem((TICKS, count, width), LOW),
            vmem((count, depth), LOW),
            vmem((count, inner), LOW),
            vmem((inner, TICKS * count), LOW),
            vmem((TICKS * count, inner), LOW),
            vmem((4, count, depth), LOW),
            vmem((4, half, depth), LOW),
            vmem((4, half, depth), LOW),
            vmem((4, chips - 1, share, depth), LOW),
            vmem((4, share, depth), LOW),
            vmem((heads, 8, width), HIGH),
            vmem((heads - 1, 8, width), HIGH),
            dma((8,)),
            dma((groups, 4)),
            dma((copies,)),
            dma((copies,)),
            dma((4, CHUNKS)),
            dma((4, CHUNKS)),
        ],
        compiler_params=pltpu.CompilerParams(
            collective_id=0, has_side_effects=True, vmem_limit_bytes=44 * 2**20
        ),
        cost_estimate=pl.CostEstimate(
            flops=52 * count * depth * inner, bytes_accessed=8 * depth * inner, transcendentals=0
        ),
    )(slots, x0, g0, fresh_x, fresh_g, gain, wq, wk, wv, wo, store)


def tail_kernel(
    wq_in, wk_in, turned, vg, ctx_turned, gcat, wq_out, wk_out, wv_out, wo_out,
    wv_grad, wo_grad, early_sem, late_sem,
):
    depth, inner = wq_in.shape
    step = min(4 * DK, inner)
    copies = []

    def out(source, target, sem):
        copies.append(pltpu.make_async_copy(source, target, sem))
        copies[-1].start()

    out(wq_in, wq_out, early_sem.at[0])
    out(wk_in, wk_out, early_sem.at[1])
    for i in range(inner // step):
        piece = slice(i * step, (i + 1) * step)
        place = pl.ds(i * step, step)
        wv_grad[:, piece] = low_dot(turned[...], vg[:, piece])
        out(wv_grad.at[:, place], wv_out.at[:, place], late_sem.at[i, 0])
        wo_grad[piece, :] = low_dot(ctx_turned[piece, :], gcat[...])
        out(wo_grad.at[place], wo_out.at[place], late_sem.at[i, 1])
    for copy in copies:
        copy.wait()


def run_tail(wq_grad, wk_grad, turned, vg, ctx_turned, gcat):
    depth, inner = wq_grad.shape
    in_vmem = pl.BlockSpec(memory_space=pltpu.VMEM)
    dma = pltpu.SemaphoreType.DMA
    wide = jax.ShapeDtypeStruct((depth, inner), LOW)
    return pl.pallas_call(
        tail_kernel,
        in_specs=[in_vmem] * 6,
        out_specs=[pl.BlockSpec(memory_space=pl.ANY)] * 4,
        out_shape=[wide, wide, wide, jax.ShapeDtypeStruct((inner, depth), LOW)],
        scratch_shapes=[
            pltpu.VMEM((depth, inner), LOW),
            pltpu.VMEM((inner, depth), LOW),
            dma((2,)),
            dma((inner // min(4 * DK, inner), 2)),
        ],
        compiler_params=pltpu.CompilerParams(vmem_limit_bytes=44 * 2**20),
        cost_estimate=pl.CostEstimate(
            flops=4 * gcat.shape[0] * depth * inner,
            bytes_accessed=8 * depth * inner,
            transcendentals=0,
        ),
    )(wq_grad, wk_grad, turned, vg, ctx_turned, gcat)


def per_device(
    section_inputs,
    section_cotangents,
    fresh_tokens,
    fresh_cotangents,
    norm_gain,
    query_weight,
    key_weight,
    value_weight,
    out_weight,
    saved_inputs,
    reload_slot,
):
    x2, g2, store, gain, *rest = run_ticks(
        reload_slot,
        section_inputs[0],
        section_cotangents[0],
        fresh_tokens,
        fresh_cotangents,
        norm_gain,
        query_weight[0],
        key_weight[0],
        value_weight[0],
        out_weight[0],
        saved_inputs[0],
    )
    grads = run_tail(*rest)
    return (x2[None], g2[None], store[None], *(grad[None] for grad in grads), gain)


def solution(mesh):
    placed = (
        P("section", None, None),
        P("section", None, None),
        P(),
        P(),
        P("section", None),
        P("section", None, "head"),
        P("section", None, "head"),
        P("section", None, "head"),
        P("section", "head", None),
        P("section", None, None, "head"),
        P(),
    )
    return jax.shard_map(
        per_device,
        mesh=mesh,
        in_specs=placed,
        out_specs=(
            P("section", None, None),
            P("section", None, None),
            P("section", None, None, "head"),
            P("section", None, "head"),
            P("section", None, "head"),
            P("section", None, "head"),
            P("section", "head", None),
            P("section", "head"),
        ),
        check_vma=False,
    )
```

```python
import functools
import math

import jax
import jax.numpy as jnp
from jax import lax
from jax.experimental import pallas as pl
from jax.experimental.pallas import tpu as pltpu
from jax.sharding import PartitionSpec as P

DK = 128
TICKS = 2
CORES = 2
EPSILON = 1e-06
SCALE = DK ** (-0.5)
ONES = (((1,), (1,)), ((), ()))
LOW = jnp.bfloat16
HIGH = jnp.float32
FORWARD_HEADS = 4
BACKWARD_HEADS = 4
CHUNKS = 4
PIECES = 4


def normalize(rows, gain_row):
    floats = rows.astype(HIGH)
    inverse = lax.rsqrt(jnp.mean(floats * floats, axis=-1, keepdims=True) + EPSILON)
    unit_rows = floats * inverse
    return ((unit_rows * gain_row).astype(LOW), unit_rows, inverse)


def dot(a, b, dims=(((1,), (0,)), ((), ()))):
    return lax.dot_general(a, b, dims, preferred_element_type=HIGH)


def low_dot(a, b, dims=(((1,), (0,)), ((), ()))):
    return dot(a, b, dims).astype(LOW)


def softmax_over(scores, axis):
    shifted = scores - jnp.max(scores, axis=axis, keepdims=True)
    exponent = jnp.exp2(shifted * (SCALE * math.log2(math.e)))
    return exponent * (1.0 / jnp.sum(exponent, axis=axis, keepdims=True))


def ticks_kernel(
    heads, sections,
    slots, x0, g0, fresh_x, fresh_g, gain_hbm, wq_hbm, wk_hbm, wv_hbm, wo_hbm, store_hbm,
    x2, g2, store_out, gain_out, wq, wk, wv, wo,
    xs, gcat, gain, store, fresh, blocks, b_full, held, shares, arrived,
    normed, normed_back, turned, ctx, ctx_turned, qg_turned, kg, vg, kept, kept_soft,
    parts, pair_in, rs_out, rs_in, hop_out, gains, gains_in,
    load_sem, weight_sem, sent, got, pair_sent, pair_got,
):
    me, section = lax.axis_index("head"), lax.axis_index("section")
    chips = heads // CORES
    core, chip = lax.rem(me, CORES), me // CORES
    partner = me + 1 - 2 * core
    chip_peers = [lax.rem(chip + d, chips) * CORES + core for d in range(1, chips)]
    mirror = sections - 1 - section
    ahead = lax.rem(section + 1, sections)
    back = lax.rem(section + sections - 1, sections)
    count, depth = x0.shape
    inner = wq.shape[1]
    half = count // CORES
    share = count // heads
    width = store.shape[2]
    chunk = depth // CHUNKS

    def aligned(start, size):
        return pl.ds(pl.multiple_of(start, size), size)

    own = aligned(core * half + chip * share, share)
    own_half = aligned(core * half, half)
    other_half = aligned((1 - core) * half, half)

    loads = [
        pltpu.make_async_copy(source, target, load_sem.at[i])
        for i, (source, target) in enumerate(
            [
                (x0, xs.at[0]),
                (gain_hbm, gain),
                (store_hbm, store),
                (g0, gcat.at[pl.ds(0, count)]),
                (fresh_x.at[0, own], fresh.at[0]),
                (fresh_g.at[0, own], fresh.at[1]),
                (fresh_x.at[1, own], fresh.at[2]),
                (fresh_g.at[1, own], fresh.at[3]),
            ]
        )
    ]
    group_width = min(FORWARD_HEADS * DK, inner)
    groups = inner // group_width
    weight_loads = []
    for i in range(groups):
        piece = pl.ds(i * group_width, group_width)
        weight_loads.append(
            [
                pltpu.make_async_copy(w_hbm.at[:, piece], w.at[:, piece], weight_sem.at[i, n])
                for n, (w_hbm, w) in enumerate(((wq_hbm, wq), (wk_hbm, wk), (wv_hbm, wv)))
            ]
        )
    out_load = pltpu.make_async_copy(wo_hbm, wo, weight_sem.at[0, 3])
    for copy in loads[:3]:
        copy.start()
    for copies in weight_loads:
        for copy in copies:
            copy.start()
    out_load.start()
    for copy in loads[3:]:
        copy.start()

    barrier = pltpu.get_barrier_semaphore()
    for d in range(1, heads):
        pl.semaphore_signal(barrier, inc=1, device_id={"head": lax.rem(me + d, heads)})
    for other in (ahead, back, mirror):
        pl.semaphore_signal(barrier, inc=1, device_id={"section": other})
    pl.semaphore_wait(barrier, heads - 1 + 3)

    sends = []

    def remote(source, target, s, r, where):
        return pltpu.make_async_remote_copy(
            src_ref=source,
            dst_ref=target,
            send_sem=s,
            recv_sem=r,
            device_id=where,
            device_id_type=pl.DeviceIdType.MESH,
        )

    counter = [0]

    def sending(source, target, where):
        i = counter[0]
        counter[0] += 1
        return remote(source, target, sent.at[i], got.at[i], where)

    def go(copy):
        copy.start()
        sends.append(copy)

    def share_of(x, target):
        for i in range(heads):
            @pl.when(me == i)
            def _():
                target[...] = x[:, i * width : (i + 1) * width]

    mirror_copies = {}

    def mirror_send(name, source, target):
        mirror_copies[name] = sending(source, target, {"section": mirror})
        go(mirror_copies[name])

    block_copies = {}

    def reload_start(t):
        held[t] = store[slots[t, mirror]]
        mirror_send(("held", t), held.at[t], blocks.at[t, core, chip])

    def reload_spread(t):
        mirror_copies["held", t].wait_recv()
        own_block = blocks.at[t, core, chip]
        block_copies[t] = [sending(own_block, own_block, {"head": peer}) for peer in chip_peers]
        for copy in block_copies[t]:
            go(copy)

    def reload_pair(t):
        for copy in block_copies[t]:
            copy.wait_recv()
        pair = sending(blocks.at[t, core], blocks.at[t, core], {"head": partner})
        block_copies[t] = [pair]
        go(pair)

    def reload_finish(t):
        block_copies[t][0].wait_recv()
        block = jnp.concatenate(
            [blocks[t, i % CORES, i // CORES] for i in range(heads)], axis=1
        )
        if t:
            first = jnp.broadcast_to(slots[0, section], block.shape)
            second = jnp.broadcast_to(slots[1, section], block.shape)
            block = jnp.where(first == second, xs[0], block)
        b_full[t] = block

    class Chain:
        def __init__(self, number, target):
            self.number, self.target = number, target
            self.tick, self.backward = number // 2, number % 2
            self.pairs, self.rs = [], []

        def part(self, j, value):
            n = self.number
            columns = pl.ds(j * chunk, chunk)
            parts[n, :, j * chunk : (j + 1) * chunk] = value.astype(LOW)
            copy = remote(
                parts.at[n, other_half, columns],
                pair_in.at[n, :, columns],
                pair_sent.at[n, j],
                pair_got.at[n, j],
                {"head": partner},
            )
            go(copy)
            self.pairs.append(copy)

        def scatter(self, j):
            n = self.number
            columns = slice(j * chunk, (j + 1) * chunk)
            self.pairs[j].wait_recv()
            total = parts[n, own_half, columns].astype(HIGH) + pair_in[n, :, columns].astype(HIGH)
            rs_out[n, :, columns] = total.astype(LOW)
            place = pl.ds(j * chunk, chunk)
            for d, peer in enumerate(chip_peers):
                rows = aligned(lax.rem(chip + d + 1, chips) * share, share)
                self.rs.append(
                    sending(
                        rs_out.at[n, rows, place], rs_in.at[n, d, :, place], {"head": peer}
                    )
                )
                go(self.rs[-1])

        def hop(self):
            n, t = self.number, self.tick
            for copy in self.rs:
                copy.wait_recv()
            mine = aligned(chip * share, share)
            total = parts[n, own, :].astype(HIGH) + pair_in[n, mine, :].astype(HIGH)
            for d in range(chips - 1):
                total += rs_in[n, d].astype(HIGH)
            if self.backward:
                normed_rows, unit_rows, inverse = normalize(b_full[t, own, :], gain[...])
                unit_grad = total * gain[...]
                along = jnp.mean(unit_grad * unit_rows, axis=-1, keepdims=True)
                upstream = gcat[aligned(t * count + core * half + chip * share, share), :]
                result = upstream.astype(HIGH) + inverse * (unit_grad - unit_rows * along)
                products = total * unit_rows
                term = products[:8]
                for start in range(8, share, 8):
                    term += products[start : start + 8]
                self.gain_term = term
                where, sender, receiver = back, section != 0, section != sections - 1
            else:
                result = xs[t, own, :].astype(HIGH) + total
                where, sender, receiver = ahead, section != sections - 1, section != 0
            hop_out[n] = result.astype(LOW)
            self.hopping = sending(hop_out.at[n], self.target(own_start, share), {"section": where})
            self.sender, self.receiver = sender, receiver

            @pl.when(sender)
            def _():
                self.hopping.start()

        def gather(self):
            block = self.target(own_start, share)

            @pl.when(self.receiver)
            def _():
                self.hopping.wait_recv()

            @pl.when(jnp.logical_not(self.receiver))
            def _():
                block[...] = fresh[self.number]

            self.ag = [sending(block, block, {"head": peer}) for peer in chip_peers]
            for copy in self.ag:
                go(copy)

        def pair(self):
            for copy in self.ag:
                copy.wait_recv()
            block = self.target(core * half, half)
            self.last = sending(block, block, {"head": partner})
            go(self.last)

        def finish(self):
            self.last.wait_recv()

        def drain(self):
            @pl.when(self.sender)
            def _():
                self.hopping.wait_send()

    own_start = core * half + chip * share
    chains = [
        Chain(0, lambda start, size: xs.at[1, aligned(start, size)]),
        Chain(1, lambda start, size: gcat.at[aligned(count + start, size)]),
        Chain(2, lambda start, size: x2.at[aligned(start, size)]),
        Chain(3, lambda start, size: g2.at[aligned(start, size)]),
    ]

    stages = {}

    def breathe(*label):
        for call in stages.pop(label, ()):
            call()

    def forward(t, before_group):
        normed[...] = normalize(xs[t], gain[...])[0]
        for i in range(groups):
            before_group(i)
            piece = slice(i * group_width, (i + 1) * group_width)
            n = normed[...]
            queries, key_rows, value_rows = (low_dot(n, w[:, piece]) for w in (wq, wk, wv))
            for start in range(0, group_width, DK):
                head = slice(start, start + DK)
                soft = softmax_over(dot(queries[:, head], key_rows[:, head], ONES), -1).astype(LOW)
                place = slice(i * group_width + start, i * group_width + start + DK)
                ctx[:, place] = low_dot(soft, value_rows[:, head])
            breathe("F", t, i)
        breathe("F", t, "heads")
        if t == 0:
            out_load.wait()
        for j in range(CHUNKS):
            chains[2 * t].part(j, dot(ctx[...], wo[:, j * chunk : (j + 1) * chunk]))
            if j:
                chains[2 * t].scatter(j - 1)

    step = min(BACKWARD_HEADS * DK, inner)
    steps = inner // step

    def start_backward(t):
        normed_back[...] = normalize(b_full[t], gain[...])[0]
        turned[:, t * count : (t + 1) * count] = normed_back[...].T

    def projected(i):
        piece = slice(i * step, (i + 1) * step)
        n = normed_back[...]
        return [low_dot(n, w[:, piece]) for w in (wq, wk, wv)]

    def recompute(t, place, q, k, v):
        tokens = slice(t * count, (t + 1) * count)
        soft = softmax_over(dot(k, q, ONES), 0)
        ctx_turned[place, tokens] = low_dot(v.T, soft.astype(LOW))
        return soft

    def differentiate(t, place, q, k, v, c, soft):
        tokens = slice(t * count, (t + 1) * count)
        soft_grad = dot(v, c, ONES)
        vg[tokens, place] = low_dot(soft.astype(LOW), c)
        inside = jnp.sum(soft * soft_grad, axis=0, keepdims=True)
        score_grad = (soft * (soft_grad - inside) * SCALE).astype(LOW)
        qg_turned[place, tokens] = low_dot(k.T, score_grad)
        kg[tokens, place] = low_dot(score_grad, q)

    def upstream_grad(t, i):
        piece = slice(i * step, (i + 1) * step)
        return low_dot(gcat[t * count : (t + 1) * count, :], wo[piece, :], ONES)

    def heads_of(i):
        for start in range(0, step, DK):
            yield slice(start, start + DK), slice(i * step + start, i * step + start + DK)

    def backward_whole(t):
        for i in range(steps):
            rows = projected(i)
            ctx_grad = upstream_grad(t, i)
            for head, place in heads_of(i):
                q, k, v = (a[:, head] for a in rows)
                soft = recompute(t, place, q, k, v)
                differentiate(t, place, q, k, v, ctx_grad[:, head], soft)
            breathe("B", t, i)

    def backward_early(t):
        for i in range(steps):
            rows = projected(i)
            for n, a in enumerate(rows):
                kept[n, :, i * step : (i + 1) * step] = a
            for head, place in heads_of(i):
                kept_soft[place.start // DK] = recompute(t, place, *(a[:, head] for a in rows))
            breathe("early", t, i)

    def backward_late(t):
        for i in range(steps):
            ctx_grad = upstream_grad(t, i)
            for head, place in heads_of(i):
                q, k, v = (kept[n, :, place] for n in range(3))
                differentiate(t, place, q, k, v, ctx_grad[:, head], kept_soft[place.start // DK])
            breathe("late", t, i)

    def normed_gradient(t):
        tokens = slice(t * count, (t + 1) * count)
        for j in range(CHUNKS):
            rows = slice(j * chunk, (j + 1) * chunk)
            grad = dot(wq[rows, :], qg_turned[:, tokens])
            grad += dot(wk[rows, :], kg[tokens, :], ONES)
            grad += dot(wv[rows, :], vg[tokens, :], ONES)
            chains[2 * t + 1].part(j, grad.T)
            if j:
                chains[2 * t + 1].scatter(j - 1)
            breathe("N", t, j)

    def at(*labels):
        def add(*calls):
            stages.setdefault(labels, []).extend(calls)
        return add

    fwd0, bwd0, fwd1, bwd1 = chains
    last, early = CHUNKS - 1, steps - 1

    loads[2].wait()
    reload_start(0)
    loads[0].wait()
    loads[1].wait()
    share_of(xs.at[0], shares.at[0])

    def first_weights(i):
        for copy in weight_loads[i]:
            copy.wait()

    def spread_first():
        reload_spread(0)
        reload_start(1)
        mirror_send(("share", 0), shares.at[0], arrived.at[0])

    def share_second():
        fwd0.finish()
        share_of(xs.at[1], shares.at[1])
        mirror_send(("share", 1), shares.at[1], arrived.at[1])

    def nearest(index, end):
        return min(index, end)

    at("F", 0, nearest(2, groups - 1))(spread_first)
    forward(0, first_weights)
    fwd0.scatter(last)
    reload_pair(0)
    for copy in loads[3:]:
        copy.wait()
    reload_finish(0)

    at("B", 0, nearest(0, early))(lambda: reload_spread(1))
    at("B", 0, nearest(1, early))(fwd0.hop)
    at("B", 0, nearest(2, early))(lambda: reload_pair(1))
    at("B", 0, nearest(3, early))(fwd0.gather)
    start_backward(0)
    backward_whole(0)
    normed_gradient(0)

    reload_finish(1)
    at("early", 1, nearest(0, early))(lambda: bwd0.scatter(last), fwd0.pair)
    at("early", 1, nearest(1, early))(share_second)
    at("early", 1, nearest(2, early))(bwd0.hop)
    start_backward(1)
    backward_early(1)

    at("F", 1, nearest(1, groups - 1))(bwd0.gather)
    forward(1, lambda i: None)
    bwd0.pair()
    fwd1.scatter(last)
    bwd0.finish()

    at("late", 1, nearest(2, early))(fwd1.hop)
    at("N", 1, 0)(fwd1.gather)
    backward_late(1)
    normed_gradient(1)

    def store_update():
        for t in range(TICKS):
            mirror_copies["share", t].wait_recv()
        first = jnp.broadcast_to(slots[0, mirror], (count, width))
        second = jnp.broadcast_to(slots[1, mirror], (count, width))
        for j in range(store.shape[0]):
            value = jnp.where(first == j, arrived[0], store[j])
            store_out[j] = jnp.where(second == j, arrived[1], value)

    gain_copies = []

    def gain_send():
        total = bwd0.gain_term + bwd1.gain_term
        for i in range(heads):
            gains[i] = total[:, i * width : (i + 1) * width]
        for d in range(1, heads):
            peer = lax.rem(me + d, heads)
            gain_copies.append(sending(gains.at[peer], gains_in.at[d - 1], {"head": peer}))
            go(gain_copies[-1])

    def gain_finish():
        total = gains[me]
        for copy in gain_copies:
            copy.wait_recv()
        for d in range(heads - 1):
            total += gains_in[d]
        gain_out[...] = jnp.sum(total, axis=0, keepdims=True)

    pieces = [slice(i * step, (i + 1) * step) for i in range(steps)]
    work = []
    for piece in pieces:
        work.append((wq, piece))
    for piece in pieces:
        work.append((wk, piece))
    for piece in pieces:
        work.append((wv, piece))
    for piece in pieces:
        work.append((wo, piece))
    total_work = len(work)

    def when(sixteenth):
        return ("W", min(sixteenth * total_work // 16, total_work - 1))

    at(*when(1))(lambda: bwd1.scatter(last), fwd1.pair)
    at(*when(5))(store_update, fwd1.finish)
    at(*when(8))(bwd1.hop, gain_send)
    at(*when(15))(bwd1.gather)
    for number, (w, piece) in enumerate(work):
        if w is wq:
            wq[:, piece] = low_dot(turned[...], qg_turned[piece, :], ONES)
        elif w is wk:
            wk[:, piece] = low_dot(turned[...], kg[:, piece])
        elif w is wv:
            wv[:, piece] = low_dot(turned[...], vg[:, piece])
        else:
            wo[piece, :] = low_dot(ctx_turned[piece, :], gcat[...])
        breathe("W", number)
    gain_finish()
    bwd1.pair()
    bwd1.finish()
    assert not stages
    for copy in sends:
        copy.wait_send()
    for chain in chains:
        chain.drain()


def run_ticks(slots, x0, g0, fresh_x, fresh_g, gain, wq, wk, wv, wo, store):
    heads, sections = lax.axis_size("head"), lax.axis_size("section")
    count, depth = x0.shape
    inner = wq.shape[1]
    slot_count, _, width = store.shape
    chips = heads // CORES
    half, share = count // CORES, count // heads
    groups = inner // min(FORWARD_HEADS * DK, inner)
    peers = chips - 1
    copies = 4 + 2 * (peers + 1) + 4 * ((CHUNKS + 1) * peers + 2) + heads - 1
    in_hbm = pl.BlockSpec(memory_space=pltpu.HBM)
    in_vmem = pl.BlockSpec(memory_space=pltpu.VMEM)
    dma = pltpu.SemaphoreType.DMA
    vmem = pltpu.VMEM
    return pl.pallas_call(
        functools.partial(ticks_kernel, heads, sections),
        in_specs=[pl.BlockSpec(memory_space=pltpu.SMEM)] + [in_hbm] * 10,
        out_specs=[in_vmem] * 8,
        out_shape=[
            vmem((count, depth), LOW),
            vmem((count, depth), LOW),
            vmem(store.shape, LOW),
            vmem((1, width), HIGH),
            vmem((depth, inner), LOW),
            vmem((depth, inner), LOW),
            vmem((depth, inner), LOW),
            vmem((inner, depth), LOW),
        ],
        scratch_shapes=[
            vmem((TICKS, count, depth), LOW),
            vmem((TICKS * count, depth), LOW),
            vmem((1, depth), HIGH),
            vmem(store.shape, LOW),
            vmem((4, share, depth), LOW),
            vmem((TICKS, CORES, chips, count, width), LOW),
            vmem((TICKS, count, depth), LOW),
            vmem((TICKS, count, width), LOW),
            vmem((TICKS, count, width), LOW),
            vmem((TICKS, count, width), LOW),
            vmem((count, depth), LOW),
            vmem((count, depth), LOW),
            vmem((depth, TICKS * count), LOW),
            vmem((count, inner), LOW),
            vmem((inner, TICKS * count), LOW),
            vmem((inner, TICKS * count), LOW),
            vmem((TICKS * count, inner), LOW),
            vmem((TICKS * count, inner), LOW),
            vmem((3, count, inner), LOW),
            vmem((inner // DK, count, count), HIGH),
            vmem((4, count, depth), LOW),
            vmem((4, half, depth), LOW),
            vmem((4, half, depth), LOW),
            vmem((4, chips - 1, share, depth), LOW),
            vmem((4, share, depth), LOW),
            vmem((heads, 8, width), HIGH),
            vmem((heads - 1, 8, width), HIGH),
            dma((8,)),
            dma((groups, 4)),
            dma((copies,)),
            dma((copies,)),
            dma((4, CHUNKS)),
            dma((4, CHUNKS)),
        ],
        compiler_params=pltpu.CompilerParams(
            collective_id=0, has_side_effects=True, vmem_limit_bytes=44 * 2**20
        ),
        cost_estimate=pl.CostEstimate(
            flops=52 * count * depth * inner, bytes_accessed=8 * depth * inner, transcendentals=0
        ),
    )(slots, x0, g0, fresh_x, fresh_g, gain, wq, wk, wv, wo, store)


def tail_kernel(*refs):
    count = len(refs) // 2
    sems = refs[-1]
    copies = []
    for i, (source, target) in enumerate(zip(refs[:count], refs[count : 2 * count])):
        rows = source.shape[0]
        parts = PIECES if rows % (16 * PIECES) == 0 and rows > 512 else 1
        size = rows // parts
        for j in range(parts):
            place = pl.ds(j * size, size)
            copies.append(
                pltpu.make_async_copy(source.at[place], target.at[place], sems.at[i, j])
            )
    for copy in copies:
        copy.start()
    for copy in copies:
        copy.wait()


def run_tail(*arrays):
    return pl.pallas_call(
        tail_kernel,
        in_specs=[pl.BlockSpec(memory_space=pltpu.VMEM)] * len(arrays),
        out_specs=[pl.BlockSpec(memory_space=pltpu.HBM)] * len(arrays),
        out_shape=[pltpu.HBM(a.shape, a.dtype) for a in arrays],
        scratch_shapes=[pltpu.SemaphoreType.DMA((len(arrays), PIECES))],
        compiler_params=pltpu.CompilerParams(vmem_limit_bytes=24 * 2**20),
    )(*arrays)


def per_device(
    section_inputs,
    section_cotangents,
    fresh_tokens,
    fresh_cotangents,
    norm_gain,
    query_weight,
    key_weight,
    value_weight,
    out_weight,
    saved_inputs,
    reload_slot,
):
    made = run_ticks(
        reload_slot,
        section_inputs[0],
        section_cotangents[0],
        fresh_tokens,
        fresh_cotangents,
        norm_gain,
        query_weight[0],
        key_weight[0],
        value_weight[0],
        out_weight[0],
        saved_inputs[0],
    )
    x2, g2, store, gain, *grads = run_tail(*made)
    return (x2[None], g2[None], store[None], *(grad[None] for grad in grads), gain)


def solution(mesh):
    placed = (
        P("section", None, None),
        P("section", None, None),
        P(),
        P(),
        P("section", None),
        P("section", None, "head"),
        P("section", None, "head"),
        P("section", None, "head"),
        P("section", "head", None),
        P("section", None, None, "head"),
        P(),
    )
    return jax.shard_map(
        per_device,
        mesh=mesh,
        in_specs=placed,
        out_specs=(
            P("section", None, None),
            P("section", None, None),
            P("section", None, None, "head"),
            P("section", None, "head"),
            P("section", None, "head"),
            P("section", None, "head"),
            P("section", "head", None),
            P("section", "head"),
        ),
        check_vma=False,
    )
```

```python
import functools
import math

import jax
import jax.numpy as jnp
from jax import lax
from jax.experimental import pallas as pl
from jax.experimental.pallas import tpu as pltpu
from jax.sharding import PartitionSpec as P

DK = 128
TICKS = 2
CORES = 2
EPSILON = 1e-06
SCALE = DK ** (-0.5)
ONES = (((1,), (1,)), ((), ()))
LOW = jnp.bfloat16
HIGH = jnp.float32
FORWARD_HEADS = (4, 4)
BACKWARD_HEADS = 4
CHUNKS = 4
PIECES = 4


def normalize(rows, gain_row):
    floats = rows.astype(HIGH)
    inverse = lax.rsqrt(jnp.mean(floats * floats, axis=-1, keepdims=True) + EPSILON)
    unit_rows = floats * inverse
    return ((unit_rows * gain_row).astype(LOW), unit_rows, inverse)


def dot(a, b, dims=(((1,), (0,)), ((), ()))):
    return lax.dot_general(a, b, dims, preferred_element_type=HIGH)


def low_dot(a, b, dims=(((1,), (0,)), ((), ()))):
    return dot(a, b, dims).astype(LOW)


def softmax_over(scores, axis):
    shifted = scores - jnp.max(scores, axis=axis, keepdims=True)
    exponent = jnp.exp2(shifted * (SCALE * math.log2(math.e)))
    return exponent * (1.0 / jnp.sum(exponent, axis=axis, keepdims=True))


def ticks_kernel(
    heads, sections,
    slots, x0, g0, fresh_x, fresh_g, gain_hbm, wq_hbm, wk_hbm, wv_hbm, wo_hbm, store_hbm,
    x2, g2, store_out, gain_out, wq, wk, wv, wo,
    xs, gcat, gain, store, fresh, blocks, b_full, held, shares, arrived,
    normed, normed_back, turned, ctx, ctx_turned, qg_turned, kg, vg, kept, kept_soft,
    parts, pair_in, rs_out, rs_in, hop_out, gains, gains_in,
    load_sem, weight_sem, sent, got, pair_sent, pair_got,
):
    me, section = lax.axis_index("head"), lax.axis_index("section")
    chips = heads // CORES
    core, chip = lax.rem(me, CORES), me // CORES
    partner = me + 1 - 2 * core
    chip_peers = [lax.rem(chip + d, chips) * CORES + core for d in range(1, chips)]
    mirror = sections - 1 - section
    ahead = lax.rem(section + 1, sections)
    back = lax.rem(section + sections - 1, sections)
    count, depth = x0.shape
    inner = wq.shape[1]
    half = count // CORES
    share = count // heads
    width = store.shape[2]
    chunk = depth // CHUNKS

    def aligned(start, size):
        return pl.ds(pl.multiple_of(start, size), size)

    own = aligned(core * half + chip * share, share)
    own_half = aligned(core * half, half)
    other_half = aligned((1 - core) * half, half)

    loads = [
        pltpu.make_async_copy(source, target, load_sem.at[i])
        for i, (source, target) in enumerate(
            [
                (x0, xs.at[0]),
                (gain_hbm, gain),
                (store_hbm, store),
                (g0, gcat.at[pl.ds(0, count)]),
                (fresh_x.at[0, own_half], fresh.at[0]),
                (fresh_g.at[0, own_half], fresh.at[1]),
                (fresh_x.at[1, own_half], fresh.at[2]),
                (fresh_g.at[1, own_half], fresh.at[3]),
            ]
        )
    ]
    group_width = min(FORWARD_HEADS[0] * DK, inner)
    groups = inner // group_width
    weight_loads = []
    for i in range(groups):
        piece = pl.ds(i * group_width, group_width)
        weight_loads.append(
            [
                pltpu.make_async_copy(w_hbm.at[:, piece], w.at[:, piece], weight_sem.at[i, n])
                for n, (w_hbm, w) in enumerate(((wq_hbm, wq), (wk_hbm, wk), (wv_hbm, wv)))
            ]
        )
    out_load = pltpu.make_async_copy(wo_hbm, wo, weight_sem.at[0, 3])
    for copy in loads[:3]:
        copy.start()
    for copies in weight_loads:
        for copy in copies:
            copy.start()
    out_load.start()
    for copy in loads[3:]:
        copy.start()

    barrier = pltpu.get_barrier_semaphore()
    for d in range(1, heads):
        pl.semaphore_signal(barrier, inc=1, device_id={"head": lax.rem(me + d, heads)})
    pl.semaphore_signal(barrier, inc=1, device_id={"section": mirror})
    for d in range(chips):
        same_core = lax.rem(chip + d, chips) * CORES + core
        for other in (ahead, back):
            pl.semaphore_signal(barrier, inc=1, device_id={"section": other, "head": same_core})
    pl.semaphore_wait(barrier, heads + 2 * chips)

    sends = []

    def remote(source, target, s, r, where):
        return pltpu.make_async_remote_copy(
            src_ref=source,
            dst_ref=target,
            send_sem=s,
            recv_sem=r,
            device_id=where,
            device_id_type=pl.DeviceIdType.MESH,
        )

    counter = [0]

    def sending(source, target, where):
        i = counter[0]
        counter[0] += 1
        return remote(source, target, sent.at[i], got.at[i], where)

    def go(copy):
        copy.start()
        sends.append(copy)

    def share_of(x, target):
        for i in range(heads):
            @pl.when(me == i)
            def _():
                target[...] = x[:, i * width : (i + 1) * width]

    mirror_copies = {}

    def mirror_send(name, source, target):
        mirror_copies[name] = sending(source, target, {"section": mirror})
        go(mirror_copies[name])

    block_copies = {}

    def reload_start(t):
        held[t] = store[slots[t, mirror]]
        mirror_send(("held", t), held.at[t], blocks.at[t, core, chip])

    def reload_spread(t):
        mirror_copies["held", t].wait_recv()
        own_block = blocks.at[t, core, chip]
        block_copies[t] = [sending(own_block, own_block, {"head": peer}) for peer in chip_peers]
        for copy in block_copies[t]:
            go(copy)

    def reload_pair(t):
        for copy in block_copies[t]:
            copy.wait_recv()
        pair = sending(blocks.at[t, core], blocks.at[t, core], {"head": partner})
        block_copies[t] = [pair]
        go(pair)

    def reload_finish(t):
        block_copies[t][0].wait_recv()
        block = jnp.concatenate(
            [blocks[t, i % CORES, i // CORES] for i in range(heads)], axis=1
        )
        if t:
            first = jnp.broadcast_to(slots[0, section], block.shape)
            second = jnp.broadcast_to(slots[1, section], block.shape)
            block = jnp.where(first == second, xs[0], block)
        b_full[t] = block

    class Chain:
        def __init__(self, number, target):
            self.number, self.target = number, target
            self.tick, self.backward = number // 2, number % 2
            self.pairs, self.rs = [], []

        def part(self, j, value):
            n = self.number
            columns = pl.ds(j * chunk, chunk)
            parts[n, :, j * chunk : (j + 1) * chunk] = value.astype(LOW)
            copy = remote(
                parts.at[n, other_half, columns],
                pair_in.at[n, :, columns],
                pair_sent.at[n, j],
                pair_got.at[n, j],
                {"head": partner},
            )
            go(copy)
            self.pairs.append(copy)

        def scatter(self, j):
            n = self.number
            columns = slice(j * chunk, (j + 1) * chunk)
            self.pairs[j].wait_recv()
            total = parts[n, own_half, columns].astype(HIGH) + pair_in[n, :, columns].astype(HIGH)
            rs_out[n, :, columns] = total.astype(LOW)
            place = pl.ds(j * chunk, chunk)
            for d, peer in enumerate(chip_peers):
                rows = aligned(lax.rem(chip + d + 1, chips) * share, share)
                self.rs.append(
                    sending(
                        rs_out.at[n, rows, place], rs_in.at[n, d, :, place], {"head": peer}
                    )
                )
                go(self.rs[-1])

        def hop(self):
            n, t = self.number, self.tick
            for copy in self.rs:
                copy.wait_recv()
            mine = aligned(chip * share, share)
            total = parts[n, own, :].astype(HIGH) + pair_in[n, mine, :].astype(HIGH)
            for d in range(chips - 1):
                total += rs_in[n, d].astype(HIGH)
            if self.backward:
                normed_rows, unit_rows, inverse = normalize(b_full[t, own, :], gain[...])
                unit_grad = total * gain[...]
                along = jnp.mean(unit_grad * unit_rows, axis=-1, keepdims=True)
                upstream = gcat[aligned(t * count + core * half + chip * share, share), :]
                result = upstream.astype(HIGH) + inverse * (unit_grad - unit_rows * along)
                products = total * unit_rows
                term = products[:8]
                for start in range(8, share, 8):
                    term += products[start : start + 8]
                self.gain_term = term
                where, sender, receiver = back, section != 0, section != sections - 1
            else:
                result = xs[t, own, :].astype(HIGH) + total
                where, sender, receiver = ahead, section != sections - 1, section != 0
            hop_out[n] = result.astype(LOW)
            self.hopping = [
                sending(
                    hop_out.at[n],
                    self.target(own_start, share),
                    {"section": where, "head": lax.rem(chip + d, chips) * CORES + core},
                )
                for d in range(1, chips + 1)
            ]
            self.sender, self.receiver = sender, receiver

            @pl.when(sender)
            def _():
                for copy in self.hopping:
                    copy.start()

        def pair(self):
            block = self.target(core * half, half)

            @pl.when(self.receiver)
            def _():
                for copy in self.hopping:
                    copy.wait_recv()

            @pl.when(jnp.logical_not(self.receiver))
            def _():
                block[...] = fresh[self.number]

            self.last = sending(block, block, {"head": partner})
            go(self.last)

        def finish(self):
            self.last.wait_recv()

        def drain(self):
            @pl.when(self.sender)
            def _():
                for copy in self.hopping:
                    copy.wait_send()

    own_start = core * half + chip * share
    chains = [
        Chain(0, lambda start, size: xs.at[1, aligned(start, size)]),
        Chain(1, lambda start, size: gcat.at[aligned(count + start, size)]),
        Chain(2, lambda start, size: x2.at[aligned(start, size)]),
        Chain(3, lambda start, size: g2.at[aligned(start, size)]),
    ]

    stages = {}

    def breathe(*label):
        for call in stages.pop(label, ()):
            call()

    def forward(t, before_group):
        group_width = min(FORWARD_HEADS[t] * DK, inner)
        normed[...] = normalize(xs[t], gain[...])[0]
        for i in range(inner // group_width):
            before_group(i)
            piece = slice(i * group_width, (i + 1) * group_width)
            n = normed[...]
            queries, key_rows, value_rows = (low_dot(n, w[:, piece]) for w in (wq, wk, wv))
            for start in range(0, group_width, DK):
                head = slice(start, start + DK)
                soft = softmax_over(dot(queries[:, head], key_rows[:, head], ONES), -1).astype(LOW)
                place = slice(i * group_width + start, i * group_width + start + DK)
                ctx[:, place] = low_dot(soft, value_rows[:, head])
            breathe("F", t, i)
        if t == 0:
            out_load.wait()
        for j in range(CHUNKS):
            chains[2 * t].part(j, dot(ctx[...], wo[:, j * chunk : (j + 1) * chunk]))
            if j:
                chains[2 * t].scatter(j - 1)

    step = min(BACKWARD_HEADS * DK, inner)
    steps = inner // step

    def start_backward(t):
        normed_back[...] = normalize(b_full[t], gain[...])[0]
        turned[:, t * count : (t + 1) * count] = normed_back[...].T

    def projected(i):
        piece = slice(i * step, (i + 1) * step)
        n = normed_back[...]
        return [low_dot(n, w[:, piece]) for w in (wq, wk, wv)]

    def recompute(t, place, q, k, v):
        tokens = slice(t * count, (t + 1) * count)
        soft = softmax_over(dot(k, q, ONES), 0)
        ctx_turned[place, tokens] = low_dot(v.T, soft.astype(LOW))
        return soft

    def differentiate(t, place, q, k, v, c, soft):
        tokens = slice(t * count, (t + 1) * count)
        soft_grad = dot(v, c, ONES)
        vg[tokens, place] = low_dot(soft.astype(LOW), c)
        inside = jnp.sum(soft * soft_grad, axis=0, keepdims=True)
        score_grad = (soft * (soft_grad - inside) * SCALE).astype(LOW)
        qg_turned[place, tokens] = low_dot(k.T, score_grad)
        kg[tokens, place] = low_dot(score_grad, q)

    def upstream_grad(t, i):
        piece = slice(i * step, (i + 1) * step)
        return low_dot(gcat[t * count : (t + 1) * count, :], wo[piece, :], ONES)

    def heads_of(i):
        for start in range(0, step, DK):
            yield slice(start, start + DK), slice(i * step + start, i * step + start + DK)

    def backward_whole(t):
        for i in range(steps):
            rows = projected(i)
            ctx_grad = upstream_grad(t, i)
            for head, place in heads_of(i):
                q, k, v = (a[:, head] for a in rows)
                soft = recompute(t, place, q, k, v)
                differentiate(t, place, q, k, v, ctx_grad[:, head], soft)
            breathe("B", t, i)

    def backward_early(t):
        for i in range(steps):
            rows = projected(i)
            for n, a in enumerate(rows):
                kept[n, :, i * step : (i + 1) * step] = a
            for head, place in heads_of(i):
                kept_soft[place.start // DK] = recompute(t, place, *(a[:, head] for a in rows))
            breathe("early", t, i)

    def backward_late(t):
        for i in range(steps):
            ctx_grad = upstream_grad(t, i)
            for head, place in heads_of(i):
                q, k, v = (kept[n, :, place] for n in range(3))
                differentiate(t, place, q, k, v, ctx_grad[:, head], kept_soft[place.start // DK])
            breathe("late", t, i)

    def normed_gradient(t):
        tokens = slice(t * count, (t + 1) * count)
        for j in range(CHUNKS):
            rows = slice(j * chunk, (j + 1) * chunk)
            grad = dot(wq[rows, :], qg_turned[:, tokens])
            grad += dot(wk[rows, :], kg[tokens, :], ONES)
            grad += dot(wv[rows, :], vg[tokens, :], ONES)
            chains[2 * t + 1].part(j, grad.T)
            if j:
                chains[2 * t + 1].scatter(j - 1)
            breathe("N", t, j)

    def at(*labels):
        def add(*calls):
            stages.setdefault(labels, []).extend(calls)
        return add

    fwd0, bwd0, fwd1, bwd1 = chains
    last, early = CHUNKS - 1, steps - 1

    loads[2].wait()
    reload_start(0)
    loads[0].wait()
    loads[1].wait()
    share_of(xs.at[0], shares.at[0])

    def first_weights(i):
        for copy in weight_loads[i]:
            copy.wait()

    def spread_first():
        reload_spread(0)
        reload_start(1)
        mirror_send(("share", 0), shares.at[0], arrived.at[0])

    def share_second():
        fwd0.finish()
        share_of(xs.at[1], shares.at[1])
        mirror_send(("share", 1), shares.at[1], arrived.at[1])

    def nearest(index, end):
        return min(index, end)

    at("F", 0, nearest(2, groups - 1))(spread_first)
    forward(0, first_weights)
    fwd0.scatter(last)
    reload_pair(0)
    for copy in loads[3:]:
        copy.wait()
    reload_finish(0)

    at("B", 0, nearest(0, early))(lambda: reload_spread(1))
    at("B", 0, nearest(1, early))(fwd0.hop)
    at("B", 0, nearest(2, early))(lambda: reload_pair(1))
    start_backward(0)
    backward_whole(0)
    normed_gradient(0)

    reload_finish(1)
    at("early", 1, nearest(0, early))(lambda: bwd0.scatter(last), fwd0.pair)
    at("early", 1, nearest(1, early))(share_second)
    at("early", 1, nearest(2, early))(bwd0.hop)
    start_backward(1)
    backward_early(1)

    forward(1, lambda i: None)
    bwd0.pair()
    fwd1.scatter(last)
    bwd0.finish()

    at("late", 1, nearest(2, early))(fwd1.hop)
    backward_late(1)
    normed_gradient(1)

    def store_update():
        for t in range(TICKS):
            mirror_copies["share", t].wait_recv()
        first = jnp.broadcast_to(slots[0, mirror], (count, width))
        second = jnp.broadcast_to(slots[1, mirror], (count, width))
        for j in range(store.shape[0]):
            value = jnp.where(first == j, arrived[0], store[j])
            store_out[j] = jnp.where(second == j, arrived[1], value)

    gain_copies = []

    def gain_send():
        total = bwd0.gain_term + bwd1.gain_term
        for i in range(heads):
            gains[i] = total[:, i * width : (i + 1) * width]
        for d in range(1, heads):
            peer = lax.rem(me + d, heads)
            gain_copies.append(sending(gains.at[peer], gains_in.at[d - 1], {"head": peer}))
            go(gain_copies[-1])

    def gain_finish():
        total = gains[me]
        for copy in gain_copies:
            copy.wait_recv()
        for d in range(heads - 1):
            total += gains_in[d]
        gain_out[...] = jnp.sum(total, axis=0, keepdims=True)

    pieces = [slice(i * step, (i + 1) * step) for i in range(steps)]
    work = []
    for piece in pieces:
        work.append((wq, piece))
    for piece in pieces:
        work.append((wk, piece))
    for piece in pieces:
        work.append((wv, piece))
    for piece in pieces:
        work.append((wo, piece))
    total_work = len(work)

    def when(sixteenth):
        return ("W", min(sixteenth * total_work // 16, total_work - 1))

    at(*when(1))(lambda: bwd1.scatter(last), fwd1.pair)
    at(*when(5))(store_update, fwd1.finish)
    at(*when(8))(bwd1.hop, gain_send)
    for number, (w, piece) in enumerate(work):
        if w is wq:
            wq[:, piece] = low_dot(turned[...], qg_turned[piece, :], ONES)
        elif w is wk:
            wk[:, piece] = low_dot(turned[...], kg[:, piece])
        elif w is wv:
            wv[:, piece] = low_dot(turned[...], vg[:, piece])
        else:
            wo[piece, :] = low_dot(ctx_turned[piece, :], gcat[...])
        breathe("W", number)
    gain_finish()
    bwd1.pair()
    bwd1.finish()
    assert not stages
    for copy in sends:
        copy.wait_send()
    for chain in chains:
        chain.drain()


def run_ticks(slots, x0, g0, fresh_x, fresh_g, gain, wq, wk, wv, wo, store):
    heads, sections = lax.axis_size("head"), lax.axis_size("section")
    count, depth = x0.shape
    inner = wq.shape[1]
    slot_count, _, width = store.shape
    chips = heads // CORES
    half, share = count // CORES, count // heads
    groups = inner // min(FORWARD_HEADS[0] * DK, inner)
    peers = chips - 1
    copies = 4 + 2 * (peers + 1) + 4 * (CHUNKS * peers + chips + 1) + heads - 1
    in_hbm = pl.BlockSpec(memory_space=pltpu.HBM)
    in_vmem = pl.BlockSpec(memory_space=pltpu.VMEM)
    dma = pltpu.SemaphoreType.DMA
    vmem = pltpu.VMEM
    return pl.pallas_call(
        functools.partial(ticks_kernel, heads, sections),
        in_specs=[pl.BlockSpec(memory_space=pltpu.SMEM)] + [in_hbm] * 10,
        out_specs=[in_vmem] * 8,
        out_shape=[
            vmem((count, depth), LOW),
            vmem((count, depth), LOW),
            vmem(store.shape, LOW),
            vmem((1, width), HIGH),
            vmem((depth, inner), LOW),
            vmem((depth, inner), LOW),
            vmem((depth, inner), LOW),
            vmem((inner, depth), LOW),
        ],
        scratch_shapes=[
            vmem((TICKS, count, depth), LOW),
            vmem((TICKS * count, depth), LOW),
            vmem((1, depth), HIGH),
            vmem(store.shape, LOW),
            vmem((4, half, depth), LOW),
            vmem((TICKS, CORES, chips, count, width), LOW),
            vmem((TICKS, count, depth), LOW),
            vmem((TICKS, count, width), LOW),
            vmem((TICKS, count, width), LOW),
            vmem((TICKS, count, width), LOW),
            vmem((count, depth), LOW),
            vmem((count, depth), LOW),
            vmem((depth, TICKS * count), LOW),
            vmem((count, inner), LOW),
            vmem((inner, TICKS * count), LOW),
            vmem((inner, TICKS * count), LOW),
            vmem((TICKS * count, inner), LOW),
            vmem((TICKS * count, inner), LOW),
            vmem((3, count, inner), LOW),
            vmem((inner // DK, count, count), HIGH),
            vmem((4, count, depth), LOW),
            vmem((4, half, depth), LOW),
            vmem((4, half, depth), LOW),
            vmem((4, chips - 1, share, depth), LOW),
            vmem((4, share, depth), LOW),
            vmem((heads, 8, width), HIGH),
            vmem((heads - 1, 8, width), HIGH),
            dma((8,)),
            dma((groups, 4)),
            dma((copies,)),
            dma((copies,)),
            dma((4, CHUNKS)),
            dma((4, CHUNKS)),
        ],
        compiler_params=pltpu.CompilerParams(
            collective_id=0, has_side_effects=True, vmem_limit_bytes=44 * 2**20
        ),
        cost_estimate=pl.CostEstimate(
            flops=52 * count * depth * inner, bytes_accessed=8 * depth * inner, transcendentals=0
        ),
    )(slots, x0, g0, fresh_x, fresh_g, gain, wq, wk, wv, wo, store)


def tail_kernel(*refs):
    count = len(refs) // 2
    sems = refs[-1]
    copies = []
    for i, (source, target) in enumerate(zip(refs[:count], refs[count : 2 * count])):
        rows = source.shape[0]
        parts = PIECES if rows % (16 * PIECES) == 0 and rows > 512 else 1
        size = rows // parts
        for j in range(parts):
            place = pl.ds(j * size, size)
            copies.append(
                pltpu.make_async_copy(source.at[place], target.at[place], sems.at[i, j])
            )
    for copy in copies:
        copy.start()
    for copy in copies:
        copy.wait()


def run_tail(*arrays):
    return pl.pallas_call(
        tail_kernel,
        in_specs=[pl.BlockSpec(memory_space=pltpu.VMEM)] * len(arrays),
        out_specs=[pl.BlockSpec(memory_space=pltpu.HBM)] * len(arrays),
        out_shape=[pltpu.HBM(a.shape, a.dtype) for a in arrays],
        scratch_shapes=[pltpu.SemaphoreType.DMA((len(arrays), PIECES))],
        compiler_params=pltpu.CompilerParams(vmem_limit_bytes=24 * 2**20),
    )(*arrays)


def per_device(
    section_inputs,
    section_cotangents,
    fresh_tokens,
    fresh_cotangents,
    norm_gain,
    query_weight,
    key_weight,
    value_weight,
    out_weight,
    saved_inputs,
    reload_slot,
):
    made = run_ticks(
        reload_slot,
        section_inputs[0],
        section_cotangents[0],
        fresh_tokens,
        fresh_cotangents,
        norm_gain,
        query_weight[0],
        key_weight[0],
        value_weight[0],
        out_weight[0],
        saved_inputs[0],
    )
    x2, g2, store, gain, *grads = run_tail(*made)
    return (x2[None], g2[None], store[None], *(grad[None] for grad in grads), gain)


def solution(mesh):
    placed = (
        P("section", None, None),
        P("section", None, None),
        P(),
        P(),
        P("section", None),
        P("section", None, "head"),
        P("section", None, "head"),
        P("section", None, "head"),
        P("section", "head", None),
        P("section", None, None, "head"),
        P(),
    )
    return jax.shard_map(
        per_device,
        mesh=mesh,
        in_specs=placed,
        out_specs=(
            P("section", None, None),
            P("section", None, None),
            P("section", None, None, "head"),
            P("section", None, "head"),
            P("section", None, "head"),
            P("section", None, "head"),
            P("section", "head", None),
            P("section", "head"),
        ),
        check_vma=False,
    )
```
